256 devices in a mesh: orb: 32 (over x_hi, z, core), gz: 8 (over x_lo, y).
Axes of the slice: x: 4 (x_hi: 2, x_lo: 2; x = x_hi * 2 + x_lo), y: 4, z: 8, core: 2. Of those that a mesh axis runs over, the one named last changes fastest.
Arguments:
- orbitals: bfloat16 [4096, 32, 16, 128], P('orb', 'gz'), may hold values from -6 to 6
- dielectric: float32 [32, 16, 128], P('gz'), may hold values from 1 to 80
- pairs: int32 [32, 2, 16, 2], P('orb'), may hold values from 0 to 127, as said below
- pair_count: int32 [32, 2], P('orb'), may hold values from 4 to 16, as said below
Outputs:
- exchange: float32 [4096, 32, 16, 128], P('orb', 'gz')
The draws below stay inside these ranges and needn't reach their ends.
Inputs may be any that keep to these rules, and one draw needn't show every extreme that they name: `pairs`: column 0 is an orbital's index within group g, column 1 within the visiting group (g - s) mod 32; slots at or beyond the block's live count hold valid indices too. Live pairs of a block; they fill slots 0 to pair_count - 1.
All inputs are finite; a program needn't handle non-finite values.
Results may differ from the reference program's by a relative error of at most 0.00055.
Values may be sent and summed in bfloat16 or wider, within the bound.
A program may use at most 128 MiB of HBM per device.

```python
import math
import jax
import jax.numpy as jnp
from jax import lax

ORB_DEV = 128
PAIRS = 16
NX = 16
NY = 128
SWEEPS = 6
STEPS = 2
GROUPS = 32
NORB = 4096
NZ = 32


def draw_pairs(key, part):
    first_key, second_key = jax.random.split(key)
    entries = jax.random.randint(first_key, (GROUPS, STEPS, PAIRS, 2), 0, ORB_DEV, dtype=jnp.int32)
    chosen_group = jax.random.randint(second_key, (), 0, GROUPS, dtype=jnp.int32)
    corner = jnp.array([[ORB_DEV - 1, 0], [0, ORB_DEV - 1]], jnp.int32)
    entries = entries.at[chosen_group, 0, 0:2, :].set(corner)
    return entries


def draw_pair_count(key, part):
    first_key, second_key, third_key = jax.random.split(jax.random.fold_in(key, 7), 3)
    counts = jax.random.randint(first_key, (GROUPS, STEPS), PAIRS // 4, PAIRS + 1, dtype=jnp.int32)
    busiest = jax.random.randint(second_key, (), 0, GROUPS, dtype=jnp.int32)
    lightest = jax.random.randint(third_key, (), 0, GROUPS, dtype=jnp.int32)
    counts = counts.at[busiest, 0].set(PAIRS)
    counts = counts.at[lightest, STEPS - 1].set(PAIRS // 4)
    return counts


def steps_of(key, shape, cuts, low, top_value):
    def one(position, blocks):
        draws = jax.random.uniform(jax.random.fold_in(jax.random.fold_in(key, 6), position), (blocks,), jnp.float32, low / len(cuts), top_value / len(cuts))
        return jnp.repeat(jnp.exp(draws), shape[position] // blocks).reshape((-1,) + (1,) * (len(shape) - position - 1))

    gain = one(*cuts[0])
    for cut in cuts[1:]:
        gain = gain * one(*cut)
    return gain


def noise(own_key, dims, deviation, limit, cuts=(), kind=jnp.bfloat16):
    values = deviation * jax.random.normal(own_key, dims, jnp.float32)
    if cuts:
        values = values * steps_of(own_key, dims, cuts, -0.22, 0.18)
    return jnp.clip(values, -limit, limit).astype(kind)


def setup_inputs(seed: int = 0) -> dict:
    key_of = jax.random.split(jax.random.key(seed), 5)
    orbitals = noise(key_of[0], (NORB, NZ, NX, NY), 1.0, 6.0, ((0, 32), (1, 8)))
    dielectric = jnp.clip(jnp.exp(math.log(80.0) - 4.3820266 * jax.random.uniform(key_of[1], (NZ, NX, NY), jnp.float32) ** steps_of(key_of[1], (NZ, NX, NY), ((0, 8),), -0.2, 0.2)), 1.0, 80.0)
    pairs = draw_pairs(jax.random.fold_in(key_of[4], 71), 0)
    pair_count = draw_pair_count(jax.random.fold_in(key_of[4], 71), 0)
    return dict(orbitals=orbitals, dielectric=dielectric, pairs=pairs, pair_count=pair_count)


near_weight = 1.0
far_weight = 0.25
screening = 0.02
coupling = 4.0 * math.pi
offsets = (-2, -1, 1, 2)


def shifted(source, axis_number, offset):
    length = source.shape[axis_number]
    widths = [(0, 0)] * source.ndim
    widths[axis_number] = (2, 2)
    padded = jnp.pad(source, widths)
    return lax.slice_in_dim(padded, 2 + offset, 2 + offset + length, axis=axis_number)


def faces_of(permittivity):
    faces = []
    diagonal = screening * permittivity
    for axis_number in range(3):
        for offset in offsets:
            weight = near_weight if abs(offset) == 1 else far_weight
            face_weight = weight * 0.5 * (permittivity + shifted(permittivity, axis_number, offset))
            faces.append((axis_number, offset, face_weight))
            diagonal = diagonal + face_weight
    return faces, diagonal


def relax(density, faces, diagonal):
    potential = jnp.zeros(density.shape, jnp.float32)
    for sweep_index in range(SWEEPS):
        summed = coupling * density
        for axis_number, offset, face_weight in faces:
            summed = summed + face_weight * shifted(potential, axis_number + 1, offset)
        potential = summed / diagonal
    return potential


def reference(orbitals, dielectric, pairs, pair_count):
    faces, diagonal = faces_of(dielectric)
    exchange = jnp.zeros(orbitals.shape, jnp.float32)
    slot_ids = jnp.arange(PAIRS, dtype=jnp.int32)

    def one_block(exchange, block_index):
        group_index = block_index // STEPS
        cycle_step = block_index % STEPS
        visitor = (group_index - cycle_step - 1) % GROUPS
        chosen = pairs[group_index, cycle_step]
        live_count = pair_count[group_index, cycle_step]
        first_rows = (group_index * ORB_DEV + chosen[:, 0]).astype(jnp.int32)
        second = (visitor * ORB_DEV + chosen[:, 1]).astype(jnp.int32)
        live_mask = (slot_ids < live_count).astype(jnp.float32)
        first_values = orbitals[first_rows].astype(jnp.float32)
        second_values = orbitals[second].astype(jnp.float32)
        potential = relax(first_values * second_values, faces, diagonal) * live_mask[:, None, None, None]
        exchange = exchange.at[first_rows].add(potential * second_values)
        exchange = exchange.at[second].add(potential * first_values)
        return exchange, None

    exchange, unused = lax.scan(one_block, exchange, jnp.arange(GROUPS * STEPS, dtype=jnp.int32))
    return exchange
```

```python
import math

import jax
import jax.numpy as jnp
from jax import lax
from jax.sharding import PartitionSpec as P

SWEEPS = 6
STEPS = 2

near_weight = 1.0
far_weight = 0.25
screening = 0.02
coupling = 4.0 * math.pi
offsets = (-2, -1, 1, 2)


def with_halo(x, axis, dim, width):
    peers, length = (lax.axis_size(axis), x.shape[dim])
    up = [(i, (i + 1) % peers) for i in range(peers - 1)]
    down = [(j, i) for i, j in up]
    last = lax.slice_in_dim(x, length - width, length, axis=dim)
    leading = lax.slice_in_dim(x, 0, width, axis=dim)
    before = lax.ppermute(last, axis, up)
    after = lax.ppermute(leading, axis, down)
    return jnp.concatenate([before, x, after], axis=dim)


def cycle(block, axis, distance):
    size = lax.axis_size(axis)
    return lax.ppermute(block, axis, [((i - distance) % size, i) for i in range(size)])


def shifted(source, axis_number, offset):
    length = source.shape[axis_number]
    widths = [(0, 0)] * source.ndim
    widths[axis_number] = (2, 2)
    padded = jnp.pad(source, widths)
    return lax.slice_in_dim(padded, 2 + offset, 2 + offset + length, axis=axis_number)


def per_device(orbitals, dielectric, pairs, pair_count):
    planes = orbitals.shape[1]
    slots = pairs.shape[2]
    rim = with_halo(dielectric, "gz", 0, 2)
    center = rim[2 : 2 + planes]
    faces = []
    diagonal = screening * center
    for axis_number in range(3):
        for offset in offsets:
            weight = near_weight if abs(offset) == 1 else far_weight
            if axis_number == 0:
                beyond = rim[2 + offset : 2 + offset + planes]
            else:
                beyond = shifted(center, axis_number, offset)
            face = weight * 0.5 * (center + beyond)
            faces.append((axis_number, offset, face))
            diagonal = diagonal + face

    firsts, seconds, wanted, masks = [], [], [], []
    slot_ids = jnp.arange(slots, dtype=jnp.int32)
    for step in range(1, STEPS + 1):
        chosen = pairs[0, step - 1]
        asked = cycle(chosen[:, 1], "orb", -step)
        wanted.append(asked)
        seconds.append(cycle(orbitals[asked], "orb", step))
        firsts.append(chosen[:, 0])
        masks.append((slot_ids < pair_count[0, step - 1]).astype(jnp.float32))
    first_rows = jnp.concatenate(firsts)
    first = orbitals[first_rows].astype(jnp.float32)
    second = jnp.concatenate(seconds).astype(jnp.float32)
    mask = jnp.concatenate(masks)[:, None, None, None]

    source = coupling * (first * second)
    potential = source / diagonal
    for sweep in range(1, SWEEPS):
        padded = with_halo(potential.astype(jnp.bfloat16), "gz", 1, 2).astype(jnp.float32)
        summed = source
        for axis_number, offset, face in faces:
            if axis_number == 0:
                neighbor = padded[:, 2 + offset : 2 + offset + planes]
            else:
                neighbor = shifted(potential, axis_number + 1, offset)
            summed = summed + face * neighbor
        potential = summed / diagonal
    potential = potential * mask

    back = potential * first
    exchange = jnp.zeros(orbitals.shape, jnp.float32).at[first_rows].add(potential * second)
    for step in range(1, STEPS + 1):
        part = cycle(back[(step - 1) * slots : step * slots], "orb", -step)
        exchange = exchange.at[wanted[step - 1]].add(part)
    return exchange


def solution(mesh):
    placed = (
        P("orb", "gz", None, None),
        P("gz", None, None),
        P("orb", None, None, None),
        P("orb", None),
    )
    return jax.shard_map(
        per_device,
        mesh=mesh,
        in_specs=placed,
        out_specs=P("orb", "gz", None, None),
        check_vma=False,
    )
```

```python
import functools
import math

import jax
import jax.numpy as jnp
from jax import lax
from jax.experimental import pallas as pl
from jax.experimental.pallas import tpu as pltpu
from jax.sharding import PartitionSpec as P

SWEEPS = 6
STEPS = 2
ROUNDS = SWEEPS - 1
LANES = 8

near_weight = 1.0
far_weight = 0.25
screening = 0.02
coupling = 4.0 * math.pi
offsets = (-2, -1, 1, 2)
MESH = pl.DeviceIdType.MESH


def step_of(batch):
    return ((batch + 1) // 2) % 2


def half_of(batch):
    return batch // 2


def relax_kernel(
    groups,
    slabs,
    orb_hbm,
    diel,
    pairs,
    count,
    pairs_hbm,
    own_out,
    vis_out,
    asked_out,
    orb,
    asked,
    rim,
    wide,
    face,
    rdiag,
    fwd,
    sec,
    nat,
    base,
    pot,
    up_snd,
    dn_snd,
    lo_rcv,
    hi_rcv,
    ret,
    own,
    load_sem,
    ask_s,
    ask_r,
    asked_sem,
    rim_s,
    rim_r,
    fwd_s,
    fwd_r,
    up_s,
    lo_r,
    dn_s,
    hi_r,
    ret_s,
    ret_r,
    own_sem,
):
    me = lax.axis_index("orb")
    gz = lax.axis_index("gz")
    planes, nx, ny = diel.shape
    batches = sec.shape[0]
    cells = planes * nx

    def group(distance):
        return lax.rem(me + distance + groups, groups)

    load = pltpu.make_async_copy(orb_hbm, orb, load_sem)
    load.start()

    barrier = pltpu.get_barrier_semaphore()
    for distance in (-2, -1, 1, 2):
        pl.semaphore_signal(
            barrier, inc=1, device_id=(group(distance), gz), device_id_type=MESH
        )

    @pl.when(gz > 0)
    def _():
        pl.semaphore_signal(barrier, inc=1, device_id=(me, gz - 1), device_id_type=MESH)

    @pl.when(gz < slabs - 1)
    def _():
        pl.semaphore_signal(barrier, inc=1, device_id=(me, gz + 1), device_id_type=MESH)

    @pl.when((gz == 0) | (gz == slabs - 1))
    def _():
        pl.semaphore_wait(barrier, 5)

    @pl.when((gz > 0) & (gz < slabs - 1))
    def _():
        pl.semaphore_wait(barrier, 6)

    def ask(step):
        return pltpu.make_async_remote_copy(
            src_ref=pairs_hbm.at[0, step],
            dst_ref=asked_out.at[step],
            send_sem=ask_s.at[step],
            recv_sem=ask_r.at[step],
            device_id=(group(-step - 1), gz),
            device_id_type=MESH,
        )

    for step in range(STEPS):
        ask(step).start()

    def rim_up():
        return pltpu.make_async_remote_copy(
            src_ref=diel.at[pl.ds(planes - 2, 2)],
            dst_ref=rim.at[0],
            send_sem=rim_s.at[0],
            recv_sem=rim_r.at[0],
            device_id=(me, gz + 1),
            device_id_type=MESH,
        )

    def rim_down():
        return pltpu.make_async_remote_copy(
            src_ref=diel.at[pl.ds(0, 2)],
            dst_ref=rim.at[1],
            send_sem=rim_s.at[1],
            recv_sem=rim_r.at[1],
            device_id=(me, gz - 1),
            device_id_type=MESH,
        )

    @pl.when(gz < slabs - 1)
    def _():
        rim_up().start()

    @pl.when(gz > 0)
    def _():
        rim_down().start()

    @pl.when(gz == 0)
    def _():
        rim[0] = jnp.zeros(rim.shape[1:], rim.dtype)
        pot[:, :, 0 : 2 * nx] = jnp.zeros((batches, 2, 2 * nx, LANES, ny), jnp.float32)

    @pl.when(gz == slabs - 1)
    def _():
        rim[1] = jnp.zeros(rim.shape[1:], rim.dtype)
        pot[:, :, (planes + 2) * nx :] = jnp.zeros(
            (batches, 2, 2 * nx, LANES, ny), jnp.float32
        )

    load.wait()

    def forward(batch):
        return pltpu.make_async_remote_copy(
            src_ref=fwd.at[batch],
            dst_ref=sec.at[batch],
            send_sem=fwd_s.at[batch],
            recv_sem=fwd_r.at[batch],
            device_id=(group(step_of(batch) + 1), gz),
            device_id_type=MESH,
        )

    def asked_copy(step):
        return pltpu.make_async_copy(
            asked_out.at[step], asked.at[step], asked_sem.at[step]
        )

    for step in range(STEPS):
        ask(step).wait_recv()
        asked_copy(step).start()
    for step in range(STEPS):
        asked_copy(step).wait()
    for batch in range(batches):
        for i in range(LANES):
            row = asked[step_of(batch), half_of(batch) * LANES + i, 1]
            fwd[batch, i] = orb[row]
    for batch in range(batches):
        forward(batch).start()

    @pl.when(gz > 0)
    def _():
        rim_up().wait_recv()

    @pl.when(gz < slabs - 1)
    def _():
        rim_down().wait_recv()

    center = diel[...]
    tall = jnp.concatenate([rim[0], center, rim[1]], axis=0)
    wide[...] = jnp.zeros(wide.shape, wide.dtype)
    wide[:, 8 : 8 + nx, :] = center
    lane = lax.broadcasted_iota(jnp.int32, center.shape, 2)
    column = lax.broadcasted_iota(jnp.int32, center.shape, 1)
    level = lax.broadcasted_iota(jnp.int32, center.shape, 0) + gz * planes
    diagonal = screening * center
    made = []
    for axis_number in range(3):
        for offset in offsets:
            weight = near_weight if abs(offset) == 1 else far_weight
            if axis_number == 0:
                beyond = tall[2 + offset : 2 + offset + planes]
                place, length = level, slabs * planes
            elif axis_number == 1:
                beyond = wide[:, 8 + offset : 8 + offset + nx, :]
                place, length = column, nx
            else:
                beyond = pltpu.roll(center, (-offset) % ny, 2)
                place, length = lane, ny
            inside = (place + offset >= 0) & (place + offset < length)
            beyond = jnp.where(inside, beyond, 0.0)
            value = weight * 0.5 * (center + beyond)
            diagonal = diagonal + value
            made.append(jnp.where(inside, value, 0.0))
    reciprocal = 1.0 / diagonal
    rdiag[...] = reciprocal
    for number, value in enumerate(made):
        face[number] = (value * reciprocal).reshape(cells, ny)

    def send_up(batch, turn):
        return pltpu.make_async_remote_copy(
            src_ref=up_snd.at[batch, turn],
            dst_ref=lo_rcv.at[batch, turn],
            send_sem=up_s.at[batch, turn],
            recv_sem=lo_r.at[batch, turn],
            device_id=(me, gz + 1),
            device_id_type=MESH,
        )

    def send_down(batch, turn):
        return pltpu.make_async_remote_copy(
            src_ref=dn_snd.at[batch, turn],
            dst_ref=hi_rcv.at[batch, turn],
            send_sem=dn_s.at[batch, turn],
            recv_sem=hi_r.at[batch, turn],
            device_id=(me, gz - 1),
            device_id_type=MESH,
        )

    def publish(batch, turn, side):
        for z in range(2):
            for x in range(0, nx, 2):
                for source, target in ((planes, up_snd), (2, dn_snd)):
                    at = (source + z) * nx + x
                    both = jnp.concatenate(
                        [pot[batch, side, at], pot[batch, side, at + 1]], axis=0
                    )
                    target[batch, turn, z, x // 2] = both.astype(jnp.bfloat16)

        @pl.when(gz < slabs - 1)
        def _():
            send_up(batch, turn).start()

        @pl.when(gz > 0)
        def _():
            send_down(batch, turn).start()

    def begin(batch):
        forward(batch).wait_recv()
        step, half = step_of(batch), half_of(batch)
        live = count[0, step]
        for i in range(LANES):
            slot = half * LANES + i
            scale = jnp.where(slot < live, coupling, 0.0).astype(jnp.float32)
            first = orb[pairs[0, step, slot, 0]].astype(jnp.float32)
            second = sec[batch, i].astype(jnp.float32)
            value = (scale * (first * second)) * rdiag[...]
            nat[i * cells : (i + 1) * cells, :] = value.reshape(cells, ny)
        for cell in range(cells):
            value = nat[pl.ds(cell, LANES, stride=cells), :]
            base[batch, cell] = value
            pot[batch, 0, 2 * nx + cell] = value
        publish(batch, 0, 0)

    def unpack(source, batch, turn, side, start):
        for z in range(2):
            for x in range(0, nx, 2):
                both = source[batch, turn, z, x // 2].astype(jnp.float32)
                at = start + z * nx + x
                pot[batch, side, at] = both[:LANES]
                pot[batch, side, at + 1] = both[LANES:]

    def sweep(batch, turn):
        side = turn % 2

        @pl.when(gz > 0)
        def _():
            send_up(batch, turn).wait_recv()
            unpack(lo_rcv, batch, turn, side, 0)

        @pl.when(gz < slabs - 1)
        def _():
            send_down(batch, turn).wait_recv()
            unpack(hi_rcv, batch, turn, side, (planes + 2) * nx)

        def plane(z, carry):
            here = (z + 2) * nx
            row = z * nx
            line = [pot[batch, side, here + x] for x in range(nx)]
            for x in range(nx):
                total = base[batch, row + x]
                number = 0
                for axis_number in range(3):
                    for offset in offsets:
                        if axis_number == 0:
                            value = pot[batch, side, here + offset * nx + x]
                        elif axis_number == 1:
                            value = line[x + offset] if 0 <= x + offset < nx else None
                        else:
                            value = pltpu.roll(line[x], (-offset) % ny, 1)
                        if value is not None:
                            total = total + face[number, pl.ds(row + x, 1), :] * value
                        number += 1
                pot[batch, 1 - side, here + x] = total
            return carry

        lax.fori_loop(0, planes, plane, 0)

        @pl.when(turn < ROUNDS - 1)
        def _():
            publish(batch, turn + 1, 1 - side)

    def give_back(batch):
        return pltpu.make_async_remote_copy(
            src_ref=ret.at[batch],
            dst_ref=vis_out.at[batch],
            send_sem=ret_s.at[batch],
            recv_sem=ret_r.at[batch],
            device_id=(group(-step_of(batch) - 1), gz),
            device_id_type=MESH,
        )

    def keep(batch):
        return pltpu.make_async_copy(own.at[batch], own_out.at[batch], own_sem.at[batch])

    def finish(batch):
        step, half = step_of(batch), half_of(batch)
        side = ROUNDS % 2
        for cell in range(cells):
            nat[pl.ds(cell, LANES, stride=cells), :] = pot[batch, side, 2 * nx + cell]
        for i in range(LANES):
            slot = half * LANES + i
            value = nat[i * cells : (i + 1) * cells, :].reshape(planes, nx, ny)
            first = orb[pairs[0, step, slot, 0]].astype(jnp.float32)
            second = sec[batch, i].astype(jnp.float32)
            ret[batch, i] = value * first
            own[batch, i] = value * second
        give_back(batch).start()
        keep(batch).start()

    def diagonal_step(d, carry):
        def one(batch, inner):
            turn = d - batch

            @pl.when(turn == 0)
            def _():
                begin(batch)

            @pl.when((turn >= 1) & (turn <= ROUNDS))
            def _():
                sweep(batch, turn - 1)

            @pl.when(turn == ROUNDS)
            def _():
                finish(batch)

            return inner

        return lax.fori_loop(0, batches, one, carry)

    lax.fori_loop(0, ROUNDS + batches, diagonal_step, 0)

    for step in range(STEPS):
        ask(step).wait_send()

    @pl.when(gz < slabs - 1)
    def _():
        rim_up().wait_send()

    @pl.when(gz > 0)
    def _():
        rim_down().wait_send()

    def drain(number, carry):
        batch, turn = number // ROUNDS, number % ROUNDS

        @pl.when(gz < slabs - 1)
        def _():
            send_up(batch, turn).wait_send()

        @pl.when(gz > 0)
        def _():
            send_down(batch, turn).wait_send()

        return carry

    lax.fori_loop(0, batches * ROUNDS, drain, 0)
    for batch in range(batches):
        forward(batch).wait_send()
        keep(batch).wait()
        give_back(batch).wait()


def scatter_kernel(pairs, asked, own, vis, out):
    out[...] = jnp.zeros(out.shape, out.dtype)
    for batch in range(own.shape[0]):
        for i in range(LANES):
            slot = half_of(batch) * LANES + i
            row = pairs[0, step_of(batch), slot, 0]
            out[row] += own[batch, i]
            row = asked[step_of(batch), slot, 1]
            out[row] += vis[batch, i]


def per_device(groups, slabs, orbitals, dielectric, pairs, pair_count):
    rows, planes, nx, ny = orbitals.shape
    slots = pairs.shape[2]
    batches = STEPS * slots // LANES
    vmem = pl.BlockSpec(memory_space=pltpu.VMEM)
    smem = pl.BlockSpec(memory_space=pltpu.SMEM)
    anywhere = pl.BlockSpec(memory_space=pl.ANY)
    slab = (batches, LANES, planes, nx, ny)
    halo = (batches, ROUNDS, 2, nx // 2, 2 * LANES, ny)
    dma = pltpu.SemaphoreType.DMA
    own, vis, asked = pl.pallas_call(
        functools.partial(relax_kernel, groups, slabs),
        out_shape=(
            jax.ShapeDtypeStruct(slab, jnp.float32),
            jax.ShapeDtypeStruct(slab, jnp.float32),
            jax.ShapeDtypeStruct(pairs.shape[1:], jnp.int32),
        ),
        in_specs=[anywhere, vmem, smem, smem, anywhere],
        out_specs=(anywhere, anywhere, anywhere),
        scratch_shapes=[
            pltpu.VMEM(orbitals.shape, orbitals.dtype),
            pltpu.SMEM(pairs.shape[1:], jnp.int32),
            pltpu.VMEM((2, 2, nx, ny), jnp.float32),
            pltpu.VMEM((planes, nx + 16, ny), jnp.float32),
            pltpu.VMEM((12, planes * nx, ny), jnp.float32),
            pltpu.VMEM((planes, nx, ny), jnp.float32),
            pltpu.VMEM(slab, jnp.bfloat16),
            pltpu.VMEM(slab, jnp.bfloat16),
            pltpu.VMEM((LANES * planes * nx, ny), jnp.float32),
            pltpu.VMEM((batches, planes * nx, LANES, ny), jnp.float32),
            pltpu.VMEM((batches, 2, (planes + 4) * nx, LANES, ny), jnp.float32),
            pltpu.VMEM(halo, jnp.bfloat16),
            pltpu.VMEM(halo, jnp.bfloat16),
            pltpu.VMEM(halo, jnp.bfloat16),
            pltpu.VMEM(halo, jnp.bfloat16),
            pltpu.VMEM(slab, jnp.float32),
            pltpu.VMEM(slab, jnp.float32),
            dma,
            dma((STEPS,)),
            dma((STEPS,)),
            dma((STEPS,)),
            dma((2,)),
            dma((2,)),
            dma((batches,)),
            dma((batches,)),
            dma((batches, ROUNDS)),
            dma((batches, ROUNDS)),
            dma((batches, ROUNDS)),
            dma((batches, ROUNDS)),
            dma((batches,)),
            dma((batches,)),
            dma((batches,)),
        ],
        compiler_params=pltpu.CompilerParams(
            collective_id=0, has_side_effects=True, vmem_limit_bytes=48 << 20
        ),
        name="relax_pairs",
    )(orbitals, dielectric, pairs, pair_count, pairs)

    block = (batches, LANES, None, nx, ny)
    return pl.pallas_call(
        scatter_kernel,
        out_shape=jax.ShapeDtypeStruct(orbitals.shape, jnp.float32),
        grid_spec=pltpu.PrefetchScalarGridSpec(
            num_scalar_prefetch=2,
            grid=(planes,),
            in_specs=[
                pl.BlockSpec(block, lambda z, *_: (0, 0, z, 0, 0)),
                pl.BlockSpec(block, lambda z, *_: (0, 0, z, 0, 0)),
            ],
            out_specs=pl.BlockSpec((rows, None, nx, ny), lambda z, *_: (0, z, 0, 0)),
        ),
        name="add_by_row",
    )(pairs, asked, own, vis)


def solution(mesh):
    placed = (
        P("orb", "gz", None, None),
        P("gz", None, None),
        P("orb", None, None, None),
        P("orb", None),
    )
    return jax.shard_map(
        functools.partial(per_device, mesh.shape["orb"], mesh.shape["gz"]),
        mesh=mesh,
        in_specs=placed,
        out_specs=P("orb", "gz", None, None),
        check_vma=False,
    )
```

```python
import functools
import math

import jax
import jax.numpy as jnp
from jax import lax
from jax.experimental import pallas as pl
from jax.experimental.pallas import tpu as pltpu
from jax.sharding import PartitionSpec as P

SWEEPS = 6
STEPS = 2
ROUNDS = SWEEPS - 1
LANES = 8

near_weight = 1.0
far_weight = 0.25
screening = 0.02
coupling = 4.0 * math.pi
offsets = (-2, -1, 1, 2)
MESH = pl.DeviceIdType.MESH


PUSHED = 2


def step_of(batch):
    return 1 if batch < PUSHED else 0


def half_of(batch):
    return batch % 2


def relax_kernel(
    groups,
    slabs,
    orb_hbm,
    diel_hbm,
    pairs_hbm,
    count_hbm,
    own,
    vis,
    asked,
    orb,
    diel,
    pairs,
    count,
    rim,
    wide,
    face,
    rdiag,
    fwd,
    sec,
    nat,
    base,
    pot,
    snd,
    rcv,
    ret,
    load_sem,
    ask_s,
    ask_r,
    rim_s,
    rim_r,
    fwd_s,
    fwd_r,
    up_s,
    up_r,
    dn_s,
    dn_r,
    ret_s,
    ret_r,
):
    me = lax.axis_index("orb")
    gz = lax.axis_index("gz")
    planes, nx, ny = diel.shape
    batches = sec.shape[0]
    cells = planes * nx

    def group(distance):
        return lax.rem(me + distance + groups, groups)

    barrier = pltpu.get_barrier_semaphore()
    for distance in (-2, -1, 1, 2):
        pl.semaphore_signal(
            barrier, inc=1, device_id=(group(distance), gz), device_id_type=MESH
        )

    @pl.when(gz > 0)
    def _():
        pl.semaphore_signal(barrier, inc=1, device_id=(me, gz - 1), device_id_type=MESH)

    @pl.when(gz < slabs - 1)
    def _():
        pl.semaphore_signal(barrier, inc=1, device_id=(me, gz + 1), device_id_type=MESH)

    loads = [
        pltpu.make_async_copy(source, target, load_sem.at[number])
        for number, (source, target) in enumerate(
            ((pairs_hbm, pairs), (count_hbm, count), (orb_hbm, orb), (diel_hbm, diel))
        )
    ]
    for load in loads:
        load.start()

    @pl.when(gz == 0)
    def _():
        rim[0] = jnp.zeros(rim.shape[1:], rim.dtype)
        pot[:, :, 0 : 2 * nx] = jnp.zeros((batches, 2, 2 * nx, LANES, ny), jnp.float32)

    @pl.when(gz == slabs - 1)
    def _():
        rim[1] = jnp.zeros(rim.shape[1:], rim.dtype)
        pot[:, :, (planes + 2) * nx :] = jnp.zeros(
            (batches, 2, 2 * nx, LANES, ny), jnp.float32
        )

    for load in loads:
        load.wait()

    for batch in range(PUSHED):
        step = step_of(batch)
        live = count[0, step]
        for i in range(LANES):
            slot = half_of(batch) * LANES + i
            value = orb[pairs[0, step, 0, slot]].astype(jnp.float32)
            keep = jnp.where(slot < live, 1.0, 0.0).astype(jnp.float32)
            fwd[batch, i] = (value * keep).astype(jnp.bfloat16)

    @pl.when((gz == 0) | (gz == slabs - 1))
    def _():
        pl.semaphore_wait(barrier, 5)

    @pl.when((gz > 0) & (gz < slabs - 1))
    def _():
        pl.semaphore_wait(barrier, 6)

    def ask(step):
        return pltpu.make_async_remote_copy(
            src_ref=pairs.at[0, step],
            dst_ref=asked.at[step],
            send_sem=ask_s.at[step],
            recv_sem=ask_r.at[step],
            device_id=(group(-step - 1), gz),
            device_id_type=MESH,
        )

    for step in range(STEPS):
        ask(step).start()

    def forward(batch):
        target = -step_of(batch) - 1 if batch < PUSHED else step_of(batch) + 1
        return pltpu.make_async_remote_copy(
            src_ref=fwd.at[batch],
            dst_ref=sec.at[batch],
            send_sem=fwd_s.at[batch],
            recv_sem=fwd_r.at[batch],
            device_id=(group(target), gz),
            device_id_type=MESH,
        )

    for batch in range(PUSHED):
        forward(batch).start()

    def rim_up():
        return pltpu.make_async_remote_copy(
            src_ref=diel.at[pl.ds(planes - 2, 2)],
            dst_ref=rim.at[0],
            send_sem=rim_s.at[0],
            recv_sem=rim_r.at[0],
            device_id=(me, gz + 1),
            device_id_type=MESH,
        )

    def rim_down():
        return pltpu.make_async_remote_copy(
            src_ref=diel.at[pl.ds(0, 2)],
            dst_ref=rim.at[1],
            send_sem=rim_s.at[1],
            recv_sem=rim_r.at[1],
            device_id=(me, gz - 1),
            device_id_type=MESH,
        )

    @pl.when(gz < slabs - 1)
    def _():
        rim_up().start()

    @pl.when(gz > 0)
    def _():
        rim_down().start()

    for step in range(STEPS):
        ask(step).wait_recv()
    for batch in range(PUSHED, batches):
        for i in range(LANES):
            slot = half_of(batch) * LANES + i
            fwd[batch, i] = orb[asked[step_of(batch), 1, slot]]
    for batch in range(PUSHED, batches):
        forward(batch).start()

    @pl.when(gz > 0)
    def _():
        rim_up().wait_recv()

    @pl.when(gz < slabs - 1)
    def _():
        rim_down().wait_recv()

    center = diel[...]
    tall = jnp.concatenate([rim[0], center, rim[1]], axis=0)
    wide[...] = jnp.zeros(wide.shape, wide.dtype)
    wide[:, 8 : 8 + nx, :] = center
    lane = lax.broadcasted_iota(jnp.int32, center.shape, 2)
    column = lax.broadcasted_iota(jnp.int32, center.shape, 1)
    level = lax.broadcasted_iota(jnp.int32, center.shape, 0) + gz * planes
    diagonal = screening * center
    made = []
    for axis_number in range(3):
        for offset in offsets:
            weight = near_weight if abs(offset) == 1 else far_weight
            if axis_number == 0:
                beyond = tall[2 + offset : 2 + offset + planes]
                place, length = level, slabs * planes
            elif axis_number == 1:
                beyond = wide[:, 8 + offset : 8 + offset + nx, :]
                place, length = column, nx
            else:
                beyond = pltpu.roll(center, (-offset) % ny, 2)
                place, length = lane, ny
            inside = (place + offset >= 0) & (place + offset < length)
            beyond = jnp.where(inside, beyond, 0.0)
            value = weight * 0.5 * (center + beyond)
            diagonal = diagonal + value
            made.append(jnp.where(inside, value, 0.0))
    reciprocal = 1.0 / diagonal
    rdiag[...] = reciprocal
    for number, value in enumerate(made):
        face[number] = (value * reciprocal).reshape(cells, ny)

    def send_up(batch, turn):
        return pltpu.make_async_remote_copy(
            src_ref=snd.at[batch, turn, 1],
            dst_ref=rcv.at[batch, turn, 0],
            send_sem=up_s.at[batch, turn],
            recv_sem=up_r.at[batch, turn],
            device_id=(me, gz + 1),
            device_id_type=MESH,
        )

    def send_down(batch, turn):
        return pltpu.make_async_remote_copy(
            src_ref=snd.at[batch, turn, 0],
            dst_ref=rcv.at[batch, turn, 1],
            send_sem=dn_s.at[batch, turn],
            recv_sem=dn_r.at[batch, turn],
            device_id=(me, gz - 1),
            device_id_type=MESH,
        )

    def publish(batch, turn):
        @pl.when(gz < slabs - 1)
        def _():
            send_up(batch, turn).start()

        @pl.when(gz > 0)
        def _():
            send_down(batch, turn).start()

    def pack(batch, turn, z, line):
        for x in range(0, nx, 2):
            both = jnp.concatenate([line[x], line[x + 1]], axis=0)
            snd[batch, turn, z // 2, z % 2, x // 2] = both.astype(jnp.bfloat16)

    def local_row(batch, i):
        slot = half_of(batch) * LANES + i
        if batch < PUSHED:
            return orb[asked[step_of(batch), 1, slot]].astype(jnp.float32)
        return orb[pairs[0, step_of(batch), 0, slot]].astype(jnp.float32)

    def begin(batch):
        forward(batch).wait_recv()
        live = count[0, step_of(batch)]
        for i in range(LANES):
            slot = half_of(batch) * LANES + i
            scale = coupling
            if batch >= PUSHED:
                scale = jnp.where(slot < live, coupling, 0.0).astype(jnp.float32)
            other = sec[batch, i].astype(jnp.float32)
            value = (scale * (local_row(batch, i) * other)) * rdiag[...]
            nat[batch, i * cells : (i + 1) * cells, :] = value.reshape(cells, ny)
        for z in range(planes):
            line = [
                nat[batch, pl.ds(z * nx + x, LANES, stride=cells), :] for x in range(nx)
            ]
            for x in range(nx):
                base[batch, z * nx + x] = line[x]
                pot[batch, 0, (2 + z) * nx + x] = line[x]
            pack(batch, 0, z, line)
        publish(batch, 0)

    def unpack(batch, turn, side, edge, start):
        for z in range(2):
            for x in range(0, nx, 2):
                both = rcv[batch, turn, edge, z, x // 2].astype(jnp.float32)
                at = start + z * nx + x
                pot[batch, side, at] = both[:LANES]
                pot[batch, side, at + 1] = both[LANES:]

    def sweep(batch, turn, last):
        side = turn % 2

        @pl.when(gz > 0)
        def _():
            send_up(batch, turn).wait_recv()
            unpack(batch, turn, side, 0, 0)

        @pl.when(gz < slabs - 1)
        def _():
            send_down(batch, turn).wait_recv()
            unpack(batch, turn, side, 1, (planes + 2) * nx)

        def plane(z, carry):
            here = (z + 2) * nx
            row = z * nx
            line = [pot[batch, side, here + x] for x in range(nx)]
            totals = []
            for x in range(nx):
                number = 0
                parts = []
                for axis_number in range(3):
                    part = None
                    for offset in offsets:
                        if axis_number == 0:
                            value = pot[batch, side, here + offset * nx + x]
                        elif axis_number == 1:
                            value = line[x + offset] if 0 <= x + offset < nx else None
                        else:
                            value = pltpu.roll(line[x], (-offset) % ny, 1)
                        if value is not None:
                            value = face[number, pl.ds(row + x, 1), :] * value
                            part = value if part is None else part + value
                        number += 1
                    parts.append(part)
                totals.append((base[batch, row + x] + parts[0]) + (parts[1] + parts[2]))
            for x in range(nx):
                pot[batch, 1 - side, here + x] = totals[x]
            if not last:
                pack(batch, turn + 1, z, totals)
            return carry

        lax.fori_loop(0, planes, plane, 0)
        if not last:
            publish(batch, turn + 1)

    def give_back(batch):
        target = step_of(batch) + 1 if batch < PUSHED else -step_of(batch) - 1
        return pltpu.make_async_remote_copy(
            src_ref=ret.at[batch],
            dst_ref=vis.at[batch],
            send_sem=ret_s.at[batch],
            recv_sem=ret_r.at[batch],
            device_id=(group(target), gz),
            device_id_type=MESH,
        )

    def finish(batch):
        side = ROUNDS % 2
        for cell in range(cells):
            nat[batch, pl.ds(cell, LANES, stride=cells), :] = pot[
                batch, side, 2 * nx + cell
            ]
        values = [
            nat[batch, i * cells : (i + 1) * cells, :].reshape(planes, nx, ny)
            for i in range(LANES)
        ]
        for i in range(LANES):
            ret[batch, i] = values[i] * local_row(batch, i)
        give_back(batch).start()
        for i in range(LANES):
            own[batch, i] = values[i] * sec[batch, i].astype(jnp.float32)

    for batch in range(batches):
        begin(batch)

    def turns(turn, carry):
        def one(batch, inner):
            sweep(batch, turn, False)
            return inner

        return lax.fori_loop(0, batches, one, carry)

    lax.fori_loop(0, ROUNDS - 1, turns, 0)
    for batch in range(batches):
        sweep(batch, ROUNDS - 1, True)
        finish(batch)

    for step in range(STEPS):
        ask(step).wait_send()

    @pl.when(gz < slabs - 1)
    def _():
        rim_up().wait_send()

    @pl.when(gz > 0)
    def _():
        rim_down().wait_send()

    def drain(number, carry):
        batch, turn = number // ROUNDS, number % ROUNDS

        @pl.when(gz < slabs - 1)
        def _():
            send_up(batch, turn).wait_send()

        @pl.when(gz > 0)
        def _():
            send_down(batch, turn).wait_send()

        return carry

    lax.fori_loop(0, batches * ROUNDS, drain, 0)
    for batch in range(batches):
        forward(batch).wait_send()
        give_back(batch).wait()


def scatter_kernel(pairs, asked, own, vis, out, acc, sem):
    planes = acc.shape[1]
    half = planes // 2
    copies = []
    for part in range(2):
        where = pl.ds(part * half, half)
        acc[:, where] = jnp.zeros((acc.shape[0], half) + acc.shape[2:], acc.dtype)
        for batch in range(own.shape[0]):
            step = step_of(batch)
            for i in range(LANES):
                slot = half_of(batch) * LANES + i
                mine, theirs = pairs[0, step, 0, slot], asked[step, 1, slot]
                kept, returned = (theirs, mine) if batch < PUSHED else (mine, theirs)
                acc[kept, where] += own[batch, i, where]
                acc[returned, where] += vis[batch, i, where]
        copy = pltpu.make_async_copy(acc.at[:, where], out.at[:, where], sem.at[part])
        copy.start()
        copies.append(copy)
    for copy in copies:
        copy.wait()


def per_device(groups, slabs, orbitals, dielectric, pairs, pair_count):
    rows, planes, nx, ny = orbitals.shape
    pairs = jnp.swapaxes(pairs, 2, 3)
    slots = pairs.shape[3]
    batches = STEPS * slots // LANES
    vmem = pl.BlockSpec(memory_space=pltpu.VMEM)
    smem = pl.BlockSpec(memory_space=pltpu.SMEM)
    hbm = pl.BlockSpec(memory_space=pltpu.HBM)
    slab = (batches, LANES, planes, nx, ny)
    halo = (batches, ROUNDS, 2, 2, nx // 2, 2 * LANES, ny)
    dma = pltpu.SemaphoreType.DMA
    own, vis, asked = pl.pallas_call(
        functools.partial(relax_kernel, groups, slabs),
        out_shape=(
            jax.ShapeDtypeStruct(slab, jnp.float32),
            jax.ShapeDtypeStruct(slab, jnp.float32),
            jax.ShapeDtypeStruct(pairs.shape[1:], jnp.int32),
        ),
        in_specs=[hbm, hbm, hbm, hbm],
        out_specs=(vmem, vmem, smem),
        scratch_shapes=[
            pltpu.VMEM(orbitals.shape, orbitals.dtype),
            pltpu.VMEM(dielectric.shape, jnp.float32),
            pltpu.SMEM(pairs.shape, jnp.int32),
            pltpu.SMEM(pair_count.shape, jnp.int32),
            pltpu.VMEM((2, 2, nx, ny), jnp.float32),
            pltpu.VMEM((planes, nx + 16, ny), jnp.float32),
            pltpu.VMEM((12, planes * nx, ny), jnp.float32),
            pltpu.VMEM((planes, nx, ny), jnp.float32),
            pltpu.VMEM(slab, jnp.bfloat16),
            pltpu.VMEM(slab, jnp.bfloat16),
            pltpu.VMEM((batches, LANES * planes * nx, ny), jnp.float32),
            pltpu.VMEM((batches, planes * nx, LANES, ny), jnp.float32),
            pltpu.VMEM((batches, 2, (planes + 4) * nx, LANES, ny), jnp.float32),
            pltpu.VMEM(halo, jnp.bfloat16),
            pltpu.VMEM(halo, jnp.bfloat16),
            pltpu.VMEM(slab, jnp.float32),
            dma((4,)),
            dma((STEPS,)),
            dma((STEPS,)),
            dma((2,)),
            dma((2,)),
            dma((batches,)),
            dma((batches,)),
            dma((batches, ROUNDS)),
            dma((batches, ROUNDS)),
            dma((batches, ROUNDS)),
            dma((batches, ROUNDS)),
            dma((batches,)),
            dma((batches,)),
        ],
        compiler_params=pltpu.CompilerParams(
            collective_id=0, has_side_effects=True, vmem_limit_bytes=48 << 20
        ),
        name="relax_pairs",
    )(orbitals, dielectric, pairs, pair_count)

    return pl.pallas_call(
        scatter_kernel,
        out_shape=jax.ShapeDtypeStruct(orbitals.shape, jnp.float32),
        in_specs=[smem, smem, vmem, vmem],
        out_specs=hbm,
        scratch_shapes=[pltpu.VMEM(orbitals.shape, jnp.float32), dma((2,))],
        compiler_params=pltpu.CompilerParams(vmem_limit_bytes=32 << 20),
        name="add_by_row",
    )(pairs, asked, own, vis)


def solution(mesh):
    placed = (
        P("orb", "gz", None, None),
        P("gz", None, None),
        P("orb", None, None, None),
        P("orb", None),
    )
    return jax.shard_map(
        functools.partial(per_device, mesh.shape["orb"], mesh.shape["gz"]),
        mesh=mesh,
        in_specs=placed,
        out_specs=P("orb", "gz", None, None),
        check_vma=False,
    )
```

```python
import functools
import math

import jax
import jax.numpy as jnp
from jax import lax
from jax.experimental import pallas as pl
from jax.experimental.pallas import tpu as pltpu
from jax.sharding import PartitionSpec as P

SWEEPS = 6
STEPS = 2
ROUNDS = SWEEPS - 1
LANES = 8

near_weight = 1.0
far_weight = 0.25
screening = 0.02
coupling = 4.0 * math.pi
offsets = (-2, -1, 1, 2)
MESH = pl.DeviceIdType.MESH


PUSHED = 2


def step_of(batch):
    return 1 - batch % 2


def half_of(batch):
    return batch // 2


def relax_kernel(
    groups,
    slabs,
    orb_hbm,
    diel_hbm,
    pairs_hbm,
    count_hbm,
    own,
    vis,
    asked,
    orb,
    diel,
    pairs,
    count,
    rim,
    wide,
    face,
    rdiag,
    fwd,
    sec,
    nat,
    base,
    pot,
    snd,
    rcv,
    ret,
    load_sem,
    ask_s,
    ask_r,
    rim_s,
    rim_r,
    fwd_s,
    fwd_r,
    up_s,
    up_r,
    dn_s,
    dn_r,
    ret_s,
    ret_r,
):
    me = lax.axis_index("orb")
    gz = lax.axis_index("gz")
    planes, nx, ny = diel.shape
    batches = sec.shape[0]
    cells = planes * nx

    def group(distance):
        return lax.rem(me + distance + groups, groups)

    barrier = pltpu.get_barrier_semaphore()
    for distance in (-2, -1, 1, 2):
        pl.semaphore_signal(
            barrier, inc=1, device_id=(group(distance), gz), device_id_type=MESH
        )

    @pl.when(gz > 0)
    def _():
        pl.semaphore_signal(barrier, inc=1, device_id=(me, gz - 1), device_id_type=MESH)

    @pl.when(gz < slabs - 1)
    def _():
        pl.semaphore_signal(barrier, inc=1, device_id=(me, gz + 1), device_id_type=MESH)

    loads = [
        pltpu.make_async_copy(source, target, load_sem.at[number])
        for number, (source, target) in enumerate(
            ((pairs_hbm, pairs), (count_hbm, count), (orb_hbm, orb), (diel_hbm, diel))
        )
    ]
    for load in loads:
        load.start()

    @pl.when(gz == 0)
    def _():
        rim[0] = jnp.zeros(rim.shape[1:], rim.dtype)
        pot[:, :, 0 : 2 * nx] = jnp.zeros((batches, 2, 2 * nx, LANES, ny), jnp.float32)

    @pl.when(gz == slabs - 1)
    def _():
        rim[1] = jnp.zeros(rim.shape[1:], rim.dtype)
        pot[:, :, (planes + 2) * nx :] = jnp.zeros(
            (batches, 2, 2 * nx, LANES, ny), jnp.float32
        )

    for load in loads:
        load.wait()

    for batch in range(PUSHED):
        step = step_of(batch)
        live = count[0, step]
        for i in range(LANES):
            slot = half_of(batch) * LANES + i
            value = orb[pairs[0, step, 0, slot]].astype(jnp.float32)
            keep = jnp.where(slot < live, 1.0, 0.0).astype(jnp.float32)
            fwd[batch, i] = (value * keep).astype(jnp.bfloat16)

    @pl.when((gz == 0) | (gz == slabs - 1))
    def _():
        pl.semaphore_wait(barrier, 5)

    @pl.when((gz > 0) & (gz < slabs - 1))
    def _():
        pl.semaphore_wait(barrier, 6)

    def ask(step):
        return pltpu.make_async_remote_copy(
            src_ref=pairs.at[0, step],
            dst_ref=asked.at[step],
            send_sem=ask_s.at[step],
            recv_sem=ask_r.at[step],
            device_id=(group(-step - 1), gz),
            device_id_type=MESH,
        )

    for step in range(STEPS):
        ask(step).start()

    def forward(batch):
        target = -step_of(batch) - 1 if batch < PUSHED else step_of(batch) + 1
        return pltpu.make_async_remote_copy(
            src_ref=fwd.at[batch],
            dst_ref=sec.at[batch],
            send_sem=fwd_s.at[batch],
            recv_sem=fwd_r.at[batch],
            device_id=(group(target), gz),
            device_id_type=MESH,
        )

    for batch in range(PUSHED):
        forward(batch).start()

    def rim_up():
        return pltpu.make_async_remote_copy(
            src_ref=diel.at[pl.ds(planes - 2, 2)],
            dst_ref=rim.at[0],
            send_sem=rim_s.at[0],
            recv_sem=rim_r.at[0],
            device_id=(me, gz + 1),
            device_id_type=MESH,
        )

    def rim_down():
        return pltpu.make_async_remote_copy(
            src_ref=diel.at[pl.ds(0, 2)],
            dst_ref=rim.at[1],
            send_sem=rim_s.at[1],
            recv_sem=rim_r.at[1],
            device_id=(me, gz - 1),
            device_id_type=MESH,
        )

    @pl.when(gz < slabs - 1)
    def _():
        rim_up().start()

    @pl.when(gz > 0)
    def _():
        rim_down().start()

    for step in range(STEPS):
        ask(step).wait_recv()
    for batch in range(PUSHED, batches):
        for i in range(LANES):
            slot = half_of(batch) * LANES + i
            fwd[batch, i] = orb[asked[step_of(batch), 1, slot]]
    for batch in range(PUSHED, batches):
        forward(batch).start()

    @pl.when(gz > 0)
    def _():
        rim_up().wait_recv()

    @pl.when(gz < slabs - 1)
    def _():
        rim_down().wait_recv()

    center = diel[...]
    tall = jnp.concatenate([rim[0], center, rim[1]], axis=0)
    wide[...] = jnp.zeros(wide.shape, wide.dtype)
    wide[:, 8 : 8 + nx, :] = center
    lane = lax.broadcasted_iota(jnp.int32, center.shape, 2)
    column = lax.broadcasted_iota(jnp.int32, center.shape, 1)
    level = lax.broadcasted_iota(jnp.int32, center.shape, 0) + gz * planes
    diagonal = screening * center
    made = []
    for axis_number in range(3):
        for offset in offsets:
            weight = near_weight if abs(offset) == 1 else far_weight
            if axis_number == 0:
                beyond = tall[2 + offset : 2 + offset + planes]
                place, length = level, slabs * planes
            elif axis_number == 1:
                beyond = wide[:, 8 + offset : 8 + offset + nx, :]
                place, length = column, nx
            else:
                beyond = pltpu.roll(center, (-offset) % ny, 2)
                place, length = lane, ny
            inside = (place + offset >= 0) & (place + offset < length)
            beyond = jnp.where(inside, beyond, 0.0)
            value = weight * 0.5 * (center + beyond)
            diagonal = diagonal + value
            made.append(jnp.where(inside, value, 0.0))
    reciprocal = 1.0 / diagonal
    rdiag[...] = reciprocal
    for number, value in enumerate(made):
        face[number] = (value * reciprocal).reshape(cells, ny)

    def send_up(batch, turn):
        return pltpu.make_async_remote_copy(
            src_ref=snd.at[batch, turn, 1],
            dst_ref=rcv.at[batch, turn, 0],
            send_sem=up_s.at[batch, turn],
            recv_sem=up_r.at[batch, turn],
            device_id=(me, gz + 1),
            device_id_type=MESH,
        )

    def send_down(batch, turn):
        return pltpu.make_async_remote_copy(
            src_ref=snd.at[batch, turn, 0],
            dst_ref=rcv.at[batch, turn, 1],
            send_sem=dn_s.at[batch, turn],
            recv_sem=dn_r.at[batch, turn],
            device_id=(me, gz - 1),
            device_id_type=MESH,
        )

    def publish(batch, turn):
        @pl.when(gz < slabs - 1)
        def _():
            send_up(batch, turn).start()

        @pl.when(gz > 0)
        def _():
            send_down(batch, turn).start()

    def pack(batch, turn, z, line):
        for x in range(0, nx, 2):
            both = jnp.concatenate([line[x], line[x + 1]], axis=0)
            snd[batch, turn, z // 2, z % 2, x // 2] = both.astype(jnp.bfloat16)

    def local_row(batch, i):
        slot = half_of(batch) * LANES + i
        if batch < PUSHED:
            return orb[asked[step_of(batch), 1, slot]].astype(jnp.float32)
        return orb[pairs[0, step_of(batch), 0, slot]].astype(jnp.float32)

    def begin(batch):
        forward(batch).wait_recv()
        live = count[0, step_of(batch)]
        for i in range(LANES):
            slot = half_of(batch) * LANES + i
            scale = coupling
            if batch >= PUSHED:
                scale = jnp.where(slot < live, coupling, 0.0).astype(jnp.float32)
            other = sec[batch, i].astype(jnp.float32)
            value = (scale * (local_row(batch, i) * other)) * rdiag[...]
            nat[batch, i * cells : (i + 1) * cells, :] = value.reshape(cells, ny)
        for z in range(planes):
            line = [
                nat[batch, pl.ds(z * nx + x, LANES, stride=cells), :] for x in range(nx)
            ]
            for x in range(nx):
                base[batch, z * nx + x] = line[x]
                pot[batch, 0, (2 + z) * nx + x] = line[x]
            pack(batch, 0, z, line)
        publish(batch, 0)

    def unpack(batch, turn, side, edge, start):
        for z in range(2):
            for x in range(0, nx, 2):
                both = rcv[batch, turn, edge, z, x // 2].astype(jnp.float32)
                at = start + z * nx + x
                pot[batch, side, at] = both[:LANES]
                pot[batch, side, at + 1] = both[LANES:]

    def sweep(batch, turn, last):
        side = turn % 2

        @pl.when(gz > 0)
        def _():
            send_up(batch, turn).wait_recv()
            unpack(batch, turn, side, 0, 0)

        @pl.when(gz < slabs - 1)
        def _():
            send_down(batch, turn).wait_recv()
            unpack(batch, turn, side, 1, (planes + 2) * nx)

        def plane(z, carry):
            here = (z + 2) * nx
            row = z * nx
            line = [pot[batch, side, here + x] for x in range(nx)]
            totals = []
            for x in range(nx):
                number = 0
                parts = []
                for axis_number in range(3):
                    part = None
                    for offset in offsets:
                        if axis_number == 0:
                            value = pot[batch, side, here + offset * nx + x]
                        elif axis_number == 1:
                            value = line[x + offset] if 0 <= x + offset < nx else None
                        else:
                            value = pltpu.roll(line[x], (-offset) % ny, 1)
                        if value is not None:
                            value = face[number, pl.ds(row + x, 1), :] * value
                            part = value if part is None else part + value
                        number += 1
                    parts.append(part)
                totals.append((base[batch, row + x] + parts[0]) + (parts[1] + parts[2]))
            for x in range(nx):
                pot[batch, 1 - side, here + x] = totals[x]
            if not last:
                pack(batch, turn + 1, z, totals)
            return carry

        lax.fori_loop(0, planes, plane, 0)
        if not last:
            publish(batch, turn + 1)

    def give_back(batch):
        target = step_of(batch) + 1 if batch < PUSHED else -step_of(batch) - 1
        return pltpu.make_async_remote_copy(
            src_ref=ret.at[batch],
            dst_ref=vis.at[batch],
            send_sem=ret_s.at[batch],
            recv_sem=ret_r.at[batch],
            device_id=(group(target), gz),
            device_id_type=MESH,
        )

    def finish(batch):
        side = ROUNDS % 2
        for cell in range(cells):
            nat[batch, pl.ds(cell, LANES, stride=cells), :] = pot[
                batch, side, 2 * nx + cell
            ]
        values = [
            nat[batch, i * cells : (i + 1) * cells, :].reshape(planes, nx, ny)
            for i in range(LANES)
        ]
        for i in range(LANES):
            ret[batch, i] = values[i] * local_row(batch, i)
        give_back(batch).start()
        for i in range(LANES):
            own[batch, i] = values[i] * sec[batch, i].astype(jnp.float32)

    for batch in range(batches):
        begin(batch)

    def turns(turn, carry):
        def one(number, inner):
            batch = jnp.where(turn == 0, number, (number % 2) * 2 + number // 2)
            sweep(batch, turn, False)
            return inner

        return lax.fori_loop(0, batches, one, carry)

    lax.fori_loop(0, ROUNDS - 1, turns, 0)
    for batch in (0, 2, 1, 3):
        sweep(batch, ROUNDS - 1, True)
        finish(batch)

    for step in range(STEPS):
        ask(step).wait_send()

    @pl.when(gz < slabs - 1)
    def _():
        rim_up().wait_send()

    @pl.when(gz > 0)
    def _():
        rim_down().wait_send()

    def drain(number, carry):
        batch, turn = number // ROUNDS, number % ROUNDS

        @pl.when(gz < slabs - 1)
        def _():
            send_up(batch, turn).wait_send()

        @pl.when(gz > 0)
        def _():
            send_down(batch, turn).wait_send()

        return carry

    lax.fori_loop(0, batches * ROUNDS, drain, 0)
    for batch in range(batches):
        forward(batch).wait_send()
        give_back(batch).wait()


def scatter_kernel(pairs, asked, own, vis, out, acc, sem):
    planes = acc.shape[1]
    half = planes // 2
    copies = []
    for part in range(2):
        where = pl.ds(part * half, half)
        acc[:, where] = jnp.zeros((acc.shape[0], half) + acc.shape[2:], acc.dtype)
        for batch in range(own.shape[0]):
            step = step_of(batch)
            for i in range(LANES):
                slot = half_of(batch) * LANES + i
                mine, theirs = pairs[0, step, 0, slot], asked[step, 1, slot]
                kept, returned = (theirs, mine) if batch < PUSHED else (mine, theirs)
                acc[kept, where] += own[batch, i, where]
                acc[returned, where] += vis[batch, i, where]
        copy = pltpu.make_async_copy(acc.at[:, where], out.at[:, where], sem.at[part])
        copy.start()
        copies.append(copy)
    for copy in copies:
        copy.wait()


def per_device(groups, slabs, orbitals, dielectric, pairs, pair_count):
    rows, planes, nx, ny = orbitals.shape
    pairs = jnp.swapaxes(pairs, 2, 3)
    slots = pairs.shape[3]
    orbitals, dielectric, pairs, pair_count = (
        pltpu.with_memory_space_constraint(array, pltpu.HBM)
        for array in (orbitals, dielectric, pairs, pair_count)
    )
    batches = STEPS * slots // LANES
    vmem = pl.BlockSpec(memory_space=pltpu.VMEM)
    smem = pl.BlockSpec(memory_space=pltpu.SMEM)
    hbm = pl.BlockSpec(memory_space=pltpu.HBM)
    slab = (batches, LANES, planes, nx, ny)
    halo = (batches, ROUNDS, 2, 2, nx // 2, 2 * LANES, ny)
    dma = pltpu.SemaphoreType.DMA
    own, vis, asked = pl.pallas_call(
        functools.partial(relax_kernel, groups, slabs),
        out_shape=(
            jax.ShapeDtypeStruct(slab, jnp.float32),
            jax.ShapeDtypeStruct(slab, jnp.float32),
            jax.ShapeDtypeStruct(pairs.shape[1:], jnp.int32),
        ),
        in_specs=[hbm, hbm, hbm, hbm],
        out_specs=(vmem, vmem, smem),
        scratch_shapes=[
            pltpu.VMEM(orbitals.shape, orbitals.dtype),
            pltpu.VMEM(dielectric.shape, jnp.float32),
            pltpu.SMEM(pairs.shape, jnp.int32),
            pltpu.SMEM(pair_count.shape, jnp.int32),
            pltpu.VMEM((2, 2, nx, ny), jnp.float32),
            pltpu.VMEM((planes, nx + 16, ny), jnp.float32),
            pltpu.VMEM((12, planes * nx, ny), jnp.float32),
            pltpu.VMEM((planes, nx, ny), jnp.float32),
            pltpu.VMEM(slab, jnp.bfloat16),
            pltpu.VMEM(slab, jnp.bfloat16),
            pltpu.VMEM((batches, LANES * planes * nx, ny), jnp.float32),
            pltpu.VMEM((batches, planes * nx, LANES, ny), jnp.float32),
            pltpu.VMEM((batches, 2, (planes + 4) * nx, LANES, ny), jnp.float32),
            pltpu.VMEM(halo, jnp.bfloat16),
            pltpu.VMEM(halo, jnp.bfloat16),
            pltpu.VMEM(slab, jnp.float32),
            dma((4,)),
            dma((STEPS,)),
            dma((STEPS,)),
            dma((2,)),
            dma((2,)),
            dma((batches,)),
            dma((batches,)),
            dma((batches, ROUNDS)),
            dma((batches, ROUNDS)),
            dma((batches, ROUNDS)),
            dma((batches, ROUNDS)),
            dma((batches,)),
            dma((batches,)),
        ],
        compiler_params=pltpu.CompilerParams(
            collective_id=0, has_side_effects=True, vmem_limit_bytes=48 << 20
        ),
        name="relax_pairs",
    )(orbitals, dielectric, pairs, pair_count)

    return pl.pallas_call(
        scatter_kernel,
        out_shape=jax.ShapeDtypeStruct(orbitals.shape, jnp.float32),
        in_specs=[smem, smem, vmem, vmem],
        out_specs=hbm,
        scratch_shapes=[pltpu.VMEM(orbitals.shape, jnp.float32), dma((2,))],
        compiler_params=pltpu.CompilerParams(vmem_limit_bytes=32 << 20),
        name="add_by_row",
    )(pairs, asked, own, vis)


def solution(mesh):
    placed = (
        P("orb", "gz", None, None),
        P("gz", None, None),
        P("orb", None, None, None),
        P("orb", None),
    )
    return jax.shard_map(
        functools.partial(per_device, mesh.shape["orb"], mesh.shape["gz"]),
        mesh=mesh,
        in_specs=placed,
        out_specs=P("orb", "gz", None, None),
        check_vma=False,
    )
```

```python
import functools
import math

import jax
import jax.numpy as jnp
from jax import lax
from jax.experimental import pallas as pl
from jax.experimental.pallas import tpu as pltpu
from jax.sharding import PartitionSpec as P

SWEEPS = 6
STEPS = 2
ROUNDS = SWEEPS - 1
LANES = 8

near_weight = 1.0
far_weight = 0.25
screening = 0.02
coupling = 4.0 * math.pi
offsets = (-2, -1, 1, 2)
MESH = pl.DeviceIdType.MESH


PUSHED = 2


def step_of(batch):
    return 1 - batch % 2


def half_of(batch):
    return batch // 2


def relax_kernel(
    groups,
    slabs,
    orb_hbm,
    diel_hbm,
    pairs_hbm,
    count_hbm,
    own,
    vis,
    asked,
    orb,
    diel,
    pairs,
    count,
    rim,
    wide,
    face,
    rdiag,
    fwd,
    sec,
    nat,
    base,
    pot,
    snd,
    rcv,
    ret,
    load_sem,
    ask_s,
    ask_r,
    rim_s,
    rim_r,
    fwd_s,
    fwd_r,
    up_s,
    up_r,
    dn_s,
    dn_r,
    ret_s,
    ret_r,
):
    me = lax.axis_index("orb")
    gz = lax.axis_index("gz")
    planes, nx, ny = diel.shape
    batches = sec.shape[0]
    cells = planes * nx

    far = (me // 2) % (groups // 4) == groups // 4 - 1

    def group(distance):
        return lax.rem(me + distance + groups, groups)

    barrier = pltpu.get_barrier_semaphore()
    for distance in (-2, -1, 1, 2):
        pl.semaphore_signal(
            barrier, inc=1, device_id=(group(distance), gz), device_id_type=MESH
        )

    @pl.when(gz > 0)
    def _():
        pl.semaphore_signal(barrier, inc=1, device_id=(me, gz - 1), device_id_type=MESH)

    @pl.when(gz < slabs - 1)
    def _():
        pl.semaphore_signal(barrier, inc=1, device_id=(me, gz + 1), device_id_type=MESH)

    loads = [
        pltpu.make_async_copy(source, target, load_sem.at[number])
        for number, (source, target) in enumerate(
            ((pairs_hbm, pairs), (count_hbm, count), (orb_hbm, orb), (diel_hbm, diel))
        )
    ]
    for load in loads:
        load.start()

    @pl.when(gz == 0)
    def _():
        rim[0] = jnp.zeros(rim.shape[1:], rim.dtype)
        pot[:, :, 0 : 2 * nx] = jnp.zeros((batches, 2, 2 * nx, LANES, ny), jnp.float32)

    @pl.when(gz == slabs - 1)
    def _():
        rim[1] = jnp.zeros(rim.shape[1:], rim.dtype)
        pot[:, :, (planes + 2) * nx :] = jnp.zeros(
            (batches, 2, 2 * nx, LANES, ny), jnp.float32
        )

    for load in loads:
        load.wait()

    for batch in range(PUSHED):
        step = step_of(batch)
        live = count[0, step]
        for i in range(LANES):
            slot = half_of(batch) * LANES + i
            value = orb[pairs[0, step, 0, slot]].astype(jnp.float32)
            keep = jnp.where(slot < live, 1.0, 0.0).astype(jnp.float32)
            fwd[batch, i] = (value * keep).astype(jnp.bfloat16)

    @pl.when((gz == 0) | (gz == slabs - 1))
    def _():
        pl.semaphore_wait(barrier, 5)

    @pl.when((gz > 0) & (gz < slabs - 1))
    def _():
        pl.semaphore_wait(barrier, 6)

    def ask(step):
        return pltpu.make_async_remote_copy(
            src_ref=pairs.at[0, step],
            dst_ref=asked.at[step],
            send_sem=ask_s.at[step],
            recv_sem=ask_r.at[step],
            device_id=(group(-step - 1), gz),
            device_id_type=MESH,
        )

    for step in range(STEPS):
        ask(step).start()

    def forward(batch):
        target = -step_of(batch) - 1 if batch < PUSHED else step_of(batch) + 1
        return pltpu.make_async_remote_copy(
            src_ref=fwd.at[batch],
            dst_ref=sec.at[batch],
            send_sem=fwd_s.at[batch],
            recv_sem=fwd_r.at[batch],
            device_id=(group(target), gz),
            device_id_type=MESH,
        )

    for batch in range(PUSHED):
        forward(batch).start()

    def rim_up():
        return pltpu.make_async_remote_copy(
            src_ref=diel.at[pl.ds(planes - 2, 2)],
            dst_ref=rim.at[0],
            send_sem=rim_s.at[0],
            recv_sem=rim_r.at[0],
            device_id=(me, gz + 1),
            device_id_type=MESH,
        )

    def rim_down():
        return pltpu.make_async_remote_copy(
            src_ref=diel.at[pl.ds(0, 2)],
            dst_ref=rim.at[1],
            send_sem=rim_s.at[1],
            recv_sem=rim_r.at[1],
            device_id=(me, gz - 1),
            device_id_type=MESH,
        )

    @pl.when(gz < slabs - 1)
    def _():
        rim_up().start()

    @pl.when(gz > 0)
    def _():
        rim_down().start()

    for step in range(STEPS):
        ask(step).wait_recv()
    for batch in range(PUSHED, batches):
        for i in range(LANES):
            slot = half_of(batch) * LANES + i
            fwd[batch, i] = orb[asked[step_of(batch), 1, slot]]
    for batch in range(PUSHED, batches):
        forward(batch).start()

    @pl.when(gz > 0)
    def _():
        rim_up().wait_recv()

    @pl.when(gz < slabs - 1)
    def _():
        rim_down().wait_recv()

    center = diel[...]
    tall = jnp.concatenate([rim[0], center, rim[1]], axis=0)
    wide[...] = jnp.zeros(wide.shape, wide.dtype)
    wide[:, 8 : 8 + nx, :] = center
    lane = lax.broadcasted_iota(jnp.int32, center.shape, 2)
    column = lax.broadcasted_iota(jnp.int32, center.shape, 1)
    level = lax.broadcasted_iota(jnp.int32, center.shape, 0) + gz * planes
    diagonal = screening * center
    made = []
    for axis_number in range(3):
        for offset in offsets:
            weight = near_weight if abs(offset) == 1 else far_weight
            if axis_number == 0:
                beyond = tall[2 + offset : 2 + offset + planes]
                place, length = level, slabs * planes
            elif axis_number == 1:
                beyond = wide[:, 8 + offset : 8 + offset + nx, :]
                place, length = column, nx
            else:
                beyond = pltpu.roll(center, (-offset) % ny, 2)
                place, length = lane, ny
            inside = (place + offset >= 0) & (place + offset < length)
            beyond = jnp.where(inside, beyond, 0.0)
            value = weight * 0.5 * (center + beyond)
            diagonal = diagonal + value
            made.append(jnp.where(inside, value, 0.0))
    reciprocal = 1.0 / diagonal
    rdiag[...] = reciprocal
    for number, value in enumerate(made):
        face[number] = (value * reciprocal).reshape(cells, ny)

    def send_up(batch, turn):
        return pltpu.make_async_remote_copy(
            src_ref=snd.at[batch, turn, 1],
            dst_ref=rcv.at[batch, turn, 0],
            send_sem=up_s.at[batch, turn],
            recv_sem=up_r.at[batch, turn],
            device_id=(me, gz + 1),
            device_id_type=MESH,
        )

    def send_down(batch, turn):
        return pltpu.make_async_remote_copy(
            src_ref=snd.at[batch, turn, 0],
            dst_ref=rcv.at[batch, turn, 1],
            send_sem=dn_s.at[batch, turn],
            recv_sem=dn_r.at[batch, turn],
            device_id=(me, gz - 1),
            device_id_type=MESH,
        )

    def publish(batch, turn):
        @pl.when(gz < slabs - 1)
        def _():
            send_up(batch, turn).start()

        @pl.when(gz > 0)
        def _():
            send_down(batch, turn).start()

    def pack(batch, turn, z, line):
        for x in range(0, nx, 2):
            both = jnp.concatenate([line[x], line[x + 1]], axis=0)
            snd[batch, turn, z // 2, z % 2, x // 2] = both.astype(jnp.bfloat16)

    def local_row(batch, i):
        slot = half_of(batch) * LANES + i
        if batch < PUSHED:
            return orb[asked[step_of(batch), 1, slot]].astype(jnp.float32)
        return orb[pairs[0, step_of(batch), 0, slot]].astype(jnp.float32)

    def begin(batch):
        forward(batch).wait_recv()
        live = count[0, step_of(batch)]
        for i in range(LANES):
            slot = half_of(batch) * LANES + i
            scale = coupling
            if batch >= PUSHED:
                scale = jnp.where(slot < live, coupling, 0.0).astype(jnp.float32)
            other = sec[batch, i].astype(jnp.float32)
            value = (scale * (local_row(batch, i) * other)) * rdiag[...]
            nat[batch, i * cells : (i + 1) * cells, :] = value.reshape(cells, ny)
        for z in range(planes):
            line = [
                nat[batch, pl.ds(z * nx + x, LANES, stride=cells), :] for x in range(nx)
            ]
            for x in range(nx):
                base[batch, z * nx + x] = line[x]
                pot[batch, 0, (2 + z) * nx + x] = line[x]
            pack(batch, 0, z, line)
        publish(batch, 0)

    def unpack(batch, turn, side, edge, start):
        for z in range(2):
            for x in range(0, nx, 2):
                both = rcv[batch, turn, edge, z, x // 2].astype(jnp.float32)
                at = start + z * nx + x
                pot[batch, side, at] = both[:LANES]
                pot[batch, side, at + 1] = both[LANES:]

    def sweep(batch, turn, last):
        side = turn % 2

        @pl.when(gz > 0)
        def _():
            send_up(batch, turn).wait_recv()
            unpack(batch, turn, side, 0, 0)

        @pl.when(gz < slabs - 1)
        def _():
            send_down(batch, turn).wait_recv()
            unpack(batch, turn, side, 1, (planes + 2) * nx)

        def plane(z, carry):
            here = (z + 2) * nx
            row = z * nx
            line = [pot[batch, side, here + x] for x in range(nx)]
            totals = []
            for x in range(nx):
                number = 0
                parts = []
                for axis_number in range(3):
                    part = None
                    for offset in offsets:
                        if axis_number == 0:
                            value = pot[batch, side, here + offset * nx + x]
                        elif axis_number == 1:
                            value = line[x + offset] if 0 <= x + offset < nx else None
                        else:
                            value = pltpu.roll(line[x], (-offset) % ny, 1)
                        if value is not None:
                            value = face[number, pl.ds(row + x, 1), :] * value
                            part = value if part is None else part + value
                        number += 1
                    parts.append(part)
                totals.append((base[batch, row + x] + parts[0]) + (parts[1] + parts[2]))
            for x in range(nx):
                pot[batch, 1 - side, here + x] = totals[x]
            if not last:
                pack(batch, turn + 1, z, totals)
            return carry

        lax.fori_loop(0, planes, plane, 0)
        if not last:
            publish(batch, turn + 1)

    def give_back(batch):
        target = step_of(batch) + 1 if batch < PUSHED else -step_of(batch) - 1
        return pltpu.make_async_remote_copy(
            src_ref=ret.at[batch],
            dst_ref=vis.at[batch],
            send_sem=ret_s.at[batch],
            recv_sem=ret_r.at[batch],
            device_id=(group(target), gz),
            device_id_type=MESH,
        )

    def finish(batch):
        side = ROUNDS % 2
        for cell in range(cells):
            nat[batch, pl.ds(cell, LANES, stride=cells), :] = pot[
                batch, side, 2 * nx + cell
            ]
        values = [
            nat[batch, i * cells : (i + 1) * cells, :].reshape(planes, nx, ny)
            for i in range(LANES)
        ]
        for i in range(LANES):
            ret[batch, i] = values[i] * local_row(batch, i)
        if batch < PUSHED:

            @pl.when(jnp.logical_not(far))
            def _():
                give_back(batch).start()

        else:
            give_back(batch).start()
        for i in range(LANES):
            own[batch, i] = values[i] * sec[batch, i].astype(jnp.float32)

    for batch in range(PUSHED):
        begin(batch)

    def early(batch, carry):
        sweep(batch, 0, False)
        return carry

    lax.fori_loop(0, PUSHED, early, 0)
    for batch in range(PUSHED, batches):
        begin(batch)

    def turns(turn, carry):
        def one(batch, inner):
            sweep(batch, turn + 1 - batch // PUSHED, False)
            return inner

        return lax.fori_loop(0, batches, one, carry)

    lax.fori_loop(0, ROUNDS - 2, turns, 0)
    for batch in range(PUSHED):
        sweep(batch, ROUNDS - 1, True)
        finish(batch)

    def late(batch, carry):
        sweep(batch, ROUNDS - 2, False)
        return carry

    lax.fori_loop(PUSHED, batches, late, 0)
    for batch in range(PUSHED, batches):
        sweep(batch, ROUNDS - 1, True)
        finish(batch)

    @pl.when(far)
    def _():
        for batch in range(PUSHED):
            give_back(batch).start()

    for step in range(STEPS):
        ask(step).wait_send()

    @pl.when(gz < slabs - 1)
    def _():
        rim_up().wait_send()

    @pl.when(gz > 0)
    def _():
        rim_down().wait_send()

    def drain(number, carry):
        batch, turn = number // ROUNDS, number % ROUNDS

        @pl.when(gz < slabs - 1)
        def _():
            send_up(batch, turn).wait_send()

        @pl.when(gz > 0)
        def _():
            send_down(batch, turn).wait_send()

        return carry

    lax.fori_loop(0, batches * ROUNDS, drain, 0)
    for batch in range(batches):
        forward(batch).wait_send()
        give_back(batch).wait()


def scatter_kernel(pairs, asked, own, vis, out, acc, sem):
    planes = acc.shape[1]
    half = planes // 2
    copies = []
    for part in range(2):
        where = pl.ds(part * half, half)
        acc[:, where] = jnp.zeros((acc.shape[0], half) + acc.shape[2:], acc.dtype)
        for batch in range(own.shape[0]):
            step = step_of(batch)
            for i in range(LANES):
                slot = half_of(batch) * LANES + i
                mine, theirs = pairs[0, step, 0, slot], asked[step, 1, slot]
                kept, returned = (theirs, mine) if batch < PUSHED else (mine, theirs)
                acc[kept, where] += own[batch, i, where]
                acc[returned, where] += vis[batch, i, where]
        copy = pltpu.make_async_copy(acc.at[:, where], out.at[:, where], sem.at[part])
        copy.start()
        copies.append(copy)
    for copy in copies:
        copy.wait()


def per_device(groups, slabs, orbitals, dielectric, pairs, pair_count):
    rows, planes, nx, ny = orbitals.shape
    pairs = jnp.swapaxes(pairs, 2, 3)
    slots = pairs.shape[3]
    orbitals, dielectric, pairs, pair_count = (
        pltpu.with_memory_space_constraint(array, pltpu.HBM)
        for array in (orbitals, dielectric, pairs, pair_count)
    )
    batches = STEPS * slots // LANES
    vmem = pl.BlockSpec(memory_space=pltpu.VMEM)
    smem = pl.BlockSpec(memory_space=pltpu.SMEM)
    hbm = pl.BlockSpec(memory_space=pltpu.HBM)
    slab = (batches, LANES, planes, nx, ny)
    halo = (batches, ROUNDS, 2, 2, nx // 2, 2 * LANES, ny)
    dma = pltpu.SemaphoreType.DMA
    own, vis, asked = pl.pallas_call(
        functools.partial(relax_kernel, groups, slabs),
        out_shape=(
            jax.ShapeDtypeStruct(slab, jnp.float32),
            jax.ShapeDtypeStruct(slab, jnp.float32),
            jax.ShapeDtypeStruct(pairs.shape[1:], jnp.int32),
        ),
        in_specs=[hbm, hbm, hbm, hbm],
        out_specs=(vmem, vmem, smem),
        scratch_shapes=[
            pltpu.VMEM(orbitals.shape, orbitals.dtype),
            pltpu.VMEM(dielectric.shape, jnp.float32),
            pltpu.SMEM(pairs.shape, jnp.int32),
            pltpu.SMEM(pair_count.shape, jnp.int32),
            pltpu.VMEM((2, 2, nx, ny), jnp.float32),
            pltpu.VMEM((planes, nx + 16, ny), jnp.float32),
            pltpu.VMEM((12, planes * nx, ny), jnp.float32),
            pltpu.VMEM((planes, nx, ny), jnp.float32),
            pltpu.VMEM(slab, jnp.bfloat16),
            pltpu.VMEM(slab, jnp.bfloat16),
            pltpu.VMEM((batches, LANES * planes * nx, ny), jnp.float32),
            pltpu.VMEM((batches, planes * nx, LANES, ny), jnp.float32),
            pltpu.VMEM((batches, 2, (planes + 4) * nx, LANES, ny), jnp.float32),
            pltpu.VMEM(halo, jnp.bfloat16),
            pltpu.VMEM(halo, jnp.bfloat16),
            pltpu.VMEM(slab, jnp.float32),
            dma((4,)),
            dma((STEPS,)),
            dma((STEPS,)),
            dma((2,)),
            dma((2,)),
            dma((batches,)),
            dma((batches,)),
            dma((batches, ROUNDS)),
            dma((batches, ROUNDS)),
            dma((batches, ROUNDS)),
            dma((batches, ROUNDS)),
            dma((batches,)),
            dma((batches,)),
        ],
        compiler_params=pltpu.CompilerParams(
            collective_id=0, has_side_effects=True, vmem_limit_bytes=48 << 20
        ),
        name="relax_pairs",
    )(orbitals, dielectric, pairs, pair_count)

    return pl.pallas_call(
        scatter_kernel,
        out_shape=jax.ShapeDtypeStruct(orbitals.shape, jnp.float32),
        in_specs=[smem, smem, vmem, vmem],
        out_specs=hbm,
        scratch_shapes=[pltpu.VMEM(orbitals.shape, jnp.float32), dma((2,))],
        compiler_params=pltpu.CompilerParams(vmem_limit_bytes=32 << 20),
        name="add_by_row",
    )(pairs, asked, own, vis)


def solution(mesh):
    placed = (
        P("orb", "gz", None, None),
        P("gz", None, None),
        P("orb", None, None, None),
        P("orb", None),
    )
    return jax.shard_map(
        functools.partial(per_device, mesh.shape["orb"], mesh.shape["gz"]),
        mesh=mesh,
        in_specs=placed,
        out_specs=P("orb", "gz", None, None),
        check_vma=False,
    )
```

```python
import functools
import math

import jax
import jax.numpy as jnp
from jax import lax
from jax.experimental import pallas as pl
from jax.experimental.pallas import tpu as pltpu
from jax.sharding import PartitionSpec as P

SWEEPS = 6
STEPS = 2
ROUNDS = SWEEPS - 1
LANES = 8

near_weight = 1.0
far_weight = 0.25
screening = 0.02
coupling = 4.0 * math.pi
offsets = (-2, -1, 1, 2)
MESH = pl.DeviceIdType.MESH


PUSHED = 2


def step_of(batch):
    return 1 - batch % 2


def half_of(batch):
    return batch // 2


def relax_kernel(
    groups,
    slabs,
    orb_hbm,
    diel_hbm,
    pairs_hbm,
    count_hbm,
    own,
    vis,
    asked,
    orb,
    diel,
    pairs,
    count,
    rim,
    wide,
    face,
    rdiag,
    fwd,
    sec,
    nat,
    base,
    pot,
    snd,
    rcv,
    ret,
    load_sem,
    ask_s,
    ask_r,
    rim_s,
    rim_r,
    fwd_s,
    fwd_r,
    up_s,
    up_r,
    dn_s,
    dn_r,
    ret_s,
    ret_r,
):
    me = lax.axis_index("orb")
    gz = lax.axis_index("gz")
    planes, nx, ny = diel.shape
    batches = sec.shape[0]
    cells = planes * nx

    far = (me // 2) % (groups // 4) == groups // 4 - 1

    near = (me // 2) % (groups // 4) == 0

    def group(distance):
        return lax.rem(me + distance + groups, groups)

    barrier = pltpu.get_barrier_semaphore()
    for distance in (-2, -1, 1, 2):
        pl.semaphore_signal(
            barrier, inc=1, device_id=(group(distance), gz), device_id_type=MESH
        )

    @pl.when(gz > 0)
    def _():
        pl.semaphore_signal(barrier, inc=1, device_id=(me, gz - 1), device_id_type=MESH)

    @pl.when(gz < slabs - 1)
    def _():
        pl.semaphore_signal(barrier, inc=1, device_id=(me, gz + 1), device_id_type=MESH)

    loads = [
        pltpu.make_async_copy(source, target, load_sem.at[number])
        for number, (source, target) in enumerate(
            ((pairs_hbm, pairs), (count_hbm, count), (orb_hbm, orb), (diel_hbm, diel))
        )
    ]
    for load in loads:
        load.start()

    @pl.when(gz == 0)
    def _():
        rim[0] = jnp.zeros(rim.shape[1:], rim.dtype)
        pot[:, :, 0 : 2 * nx] = jnp.zeros((batches, 2, 2 * nx, LANES, ny), jnp.float32)

    @pl.when(gz == slabs - 1)
    def _():
        rim[1] = jnp.zeros(rim.shape[1:], rim.dtype)
        pot[:, :, (planes + 2) * nx :] = jnp.zeros(
            (batches, 2, 2 * nx, LANES, ny), jnp.float32
        )

    for load in loads:
        load.wait()

    for batch in range(PUSHED):
        step = step_of(batch)
        live = count[0, step]
        for i in range(LANES):
            slot = half_of(batch) * LANES + i
            value = orb[pairs[0, step, 0, slot]].astype(jnp.float32)
            keep = jnp.where(slot < live, 1.0, 0.0).astype(jnp.float32)
            fwd[batch, i] = (value * keep).astype(jnp.bfloat16)

    @pl.when((gz == 0) | (gz == slabs - 1))
    def _():
        pl.semaphore_wait(barrier, 5)

    @pl.when((gz > 0) & (gz < slabs - 1))
    def _():
        pl.semaphore_wait(barrier, 6)

    def ask(step):
        return pltpu.make_async_remote_copy(
            src_ref=pairs.at[0, step],
            dst_ref=asked.at[step],
            send_sem=ask_s.at[step],
            recv_sem=ask_r.at[step],
            device_id=(group(-step - 1), gz),
            device_id_type=MESH,
        )

    for step in range(STEPS):
        ask(step).start()

    def forward(batch):
        target = -step_of(batch) - 1 if batch < PUSHED else step_of(batch) + 1
        return pltpu.make_async_remote_copy(
            src_ref=fwd.at[batch],
            dst_ref=sec.at[batch],
            send_sem=fwd_s.at[batch],
            recv_sem=fwd_r.at[batch],
            device_id=(group(target), gz),
            device_id_type=MESH,
        )

    for batch in range(PUSHED):
        forward(batch).start()

    def rim_up():
        return pltpu.make_async_remote_copy(
            src_ref=diel.at[pl.ds(planes - 2, 2)],
            dst_ref=rim.at[0],
            send_sem=rim_s.at[0],
            recv_sem=rim_r.at[0],
            device_id=(me, gz + 1),
            device_id_type=MESH,
        )

    def rim_down():
        return pltpu.make_async_remote_copy(
            src_ref=diel.at[pl.ds(0, 2)],
            dst_ref=rim.at[1],
            send_sem=rim_s.at[1],
            recv_sem=rim_r.at[1],
            device_id=(me, gz - 1),
            device_id_type=MESH,
        )

    @pl.when(gz < slabs - 1)
    def _():
        rim_up().start()

    @pl.when(gz > 0)
    def _():
        rim_down().start()

    for step in range(STEPS):
        ask(step).wait_recv()
    for batch in range(PUSHED, batches):
        for i in range(LANES):
            slot = half_of(batch) * LANES + i
            fwd[batch, i] = orb[asked[step_of(batch), 1, slot]]
    for batch in range(PUSHED, batches):
        forward(batch).start()

    @pl.when(gz > 0)
    def _():
        rim_up().wait_recv()

    @pl.when(gz < slabs - 1)
    def _():
        rim_down().wait_recv()

    center = diel[...]
    tall = jnp.concatenate([rim[0], center, rim[1]], axis=0)
    wide[...] = jnp.zeros(wide.shape, wide.dtype)
    wide[:, 8 : 8 + nx, :] = center
    lane = lax.broadcasted_iota(jnp.int32, center.shape, 2)
    column = lax.broadcasted_iota(jnp.int32, center.shape, 1)
    level = lax.broadcasted_iota(jnp.int32, center.shape, 0) + gz * planes
    diagonal = screening * center
    made = []
    for axis_number in range(3):
        for offset in offsets:
            weight = near_weight if abs(offset) == 1 else far_weight
            if axis_number == 0:
                beyond = tall[2 + offset : 2 + offset + planes]
                place, length = level, slabs * planes
            elif axis_number == 1:
                beyond = wide[:, 8 + offset : 8 + offset + nx, :]
                place, length = column, nx
            else:
                beyond = pltpu.roll(center, (-offset) % ny, 2)
                place, length = lane, ny
            inside = (place + offset >= 0) & (place + offset < length)
            beyond = jnp.where(inside, beyond, 0.0)
            value = weight * 0.5 * (center + beyond)
            diagonal = diagonal + value
            made.append(jnp.where(inside, value, 0.0))
    reciprocal = 1.0 / diagonal
    rdiag[...] = reciprocal
    for number, value in enumerate(made):
        face[number] = (value * reciprocal).reshape(cells, ny)

    def send_up(batch, turn):
        return pltpu.make_async_remote_copy(
            src_ref=snd.at[batch, turn, 1],
            dst_ref=rcv.at[batch, turn, 0],
            send_sem=up_s.at[batch, turn],
            recv_sem=up_r.at[batch, turn],
            device_id=(me, gz + 1),
            device_id_type=MESH,
        )

    def send_down(batch, turn):
        return pltpu.make_async_remote_copy(
            src_ref=snd.at[batch, turn, 0],
            dst_ref=rcv.at[batch, turn, 1],
            send_sem=dn_s.at[batch, turn],
            recv_sem=dn_r.at[batch, turn],
            device_id=(me, gz - 1),
            device_id_type=MESH,
        )

    def publish(batch, turn):
        @pl.when(gz < slabs - 1)
        def _():
            send_up(batch, turn).start()

        @pl.when(gz > 0)
        def _():
            send_down(batch, turn).start()

    def pack(batch, turn, z, line):
        for x in range(0, nx, 2):
            both = jnp.concatenate([line[x], line[x + 1]], axis=0)
            snd[batch, turn, z // 2, z % 2, x // 2] = both.astype(jnp.bfloat16)

    def local_row(batch, i):
        slot = half_of(batch) * LANES + i
        if batch < PUSHED:
            return orb[asked[step_of(batch), 1, slot]].astype(jnp.float32)
        return orb[pairs[0, step_of(batch), 0, slot]].astype(jnp.float32)

    def begin(batch):
        forward(batch).wait_recv()
        live = count[0, step_of(batch)]
        for i in range(LANES):
            slot = half_of(batch) * LANES + i
            scale = coupling
            if batch >= PUSHED:
                scale = jnp.where(slot < live, coupling, 0.0).astype(jnp.float32)
            other = sec[batch, i].astype(jnp.float32)
            value = (scale * (local_row(batch, i) * other)) * rdiag[...]
            nat[batch, i * cells : (i + 1) * cells, :] = value.reshape(cells, ny)
        for z in range(planes):
            line = [
                nat[batch, pl.ds(z * nx + x, LANES, stride=cells), :] for x in range(nx)
            ]
            for x in range(nx):
                base[batch, z * nx + x] = line[x]
                pot[batch, 0, (2 + z) * nx + x] = line[x]
            pack(batch, 0, z, line)
        publish(batch, 0)

    def unpack(batch, turn, side, edge, start):
        for z in range(2):
            for x in range(0, nx, 2):
                both = rcv[batch, turn, edge, z, x // 2].astype(jnp.float32)
                at = start + z * nx + x
                pot[batch, side, at] = both[:LANES]
                pot[batch, side, at + 1] = both[LANES:]

    def sweep(batch, turn, last):
        side = turn % 2

        @pl.when(gz > 0)
        def _():
            send_up(batch, turn).wait_recv()
            unpack(batch, turn, side, 0, 0)

        @pl.when(gz < slabs - 1)
        def _():
            send_down(batch, turn).wait_recv()
            unpack(batch, turn, side, 1, (planes + 2) * nx)

        def plane(z, carry):
            here = (z + 2) * nx
            row = z * nx
            line = [pot[batch, side, here + x] for x in range(nx)]
            totals = []
            for x in range(nx):
                number = 0
                parts = []
                for axis_number in range(3):
                    part = None
                    for offset in offsets:
                        if axis_number == 0:
                            value = pot[batch, side, here + offset * nx + x]
                        elif axis_number == 1:
                            value = line[x + offset] if 0 <= x + offset < nx else None
                        else:
                            value = pltpu.roll(line[x], (-offset) % ny, 1)
                        if value is not None:
                            value = face[number, pl.ds(row + x, 1), :] * value
                            part = value if part is None else part + value
                        number += 1
                    parts.append(part)
                totals.append((base[batch, row + x] + parts[0]) + (parts[1] + parts[2]))
            for x in range(nx):
                pot[batch, 1 - side, here + x] = totals[x]
            if not last:
                pack(batch, turn + 1, z, totals)
            return carry

        lax.fori_loop(0, planes, plane, 0)
        if not last:
            publish(batch, turn + 1)

    def give_back(batch):
        target = step_of(batch) + 1 if batch < PUSHED else -step_of(batch) - 1
        return pltpu.make_async_remote_copy(
            src_ref=ret.at[batch],
            dst_ref=vis.at[batch],
            send_sem=ret_s.at[batch],
            recv_sem=ret_r.at[batch],
            device_id=(group(target), gz),
            device_id_type=MESH,
        )

    def finish(batch):
        side = ROUNDS % 2
        for cell in range(cells):
            nat[batch, pl.ds(cell, LANES, stride=cells), :] = pot[
                batch, side, 2 * nx + cell
            ]
        values = [
            nat[batch, i * cells : (i + 1) * cells, :].reshape(planes, nx, ny)
            for i in range(LANES)
        ]
        for i in range(LANES):
            ret[batch, i] = values[i] * local_row(batch, i)
        if batch < PUSHED:

            @pl.when(jnp.logical_not(far))
            def _():
                give_back(batch).start()

        elif batch == PUSHED:

            @pl.when(jnp.logical_not(near))
            def _():
                give_back(batch).start()

        else:
            give_back(batch).start()
        for i in range(LANES):
            own[batch, i] = values[i] * sec[batch, i].astype(jnp.float32)

    for batch in range(PUSHED):
        begin(batch)

    def early(batch, carry):
        sweep(batch, 0, False)
        return carry

    lax.fori_loop(0, PUSHED, early, 0)
    for batch in range(PUSHED, batches):
        begin(batch)

    def turns(turn, carry):
        def one(batch, inner):
            sweep(batch, turn + 1 - batch // PUSHED, False)
            return inner

        return lax.fori_loop(0, batches, one, carry)

    lax.fori_loop(0, ROUNDS - 2, turns, 0)
    for batch in range(PUSHED):
        sweep(batch, ROUNDS - 1, True)
        finish(batch)

    def late(batch, carry):
        sweep(batch, ROUNDS - 2, False)
        return carry

    lax.fori_loop(PUSHED, batches, late, 0)
    for batch in range(PUSHED, batches):
        sweep(batch, ROUNDS - 1, True)
        finish(batch)

    @pl.when(far)
    def _():
        for batch in range(PUSHED):
            give_back(batch).start()

    @pl.when(near)
    def _():
        give_back(PUSHED).start()

    for step in range(STEPS):
        ask(step).wait_send()

    @pl.when(gz < slabs - 1)
    def _():
        rim_up().wait_send()

    @pl.when(gz > 0)
    def _():
        rim_down().wait_send()

    def drain(number, carry):
        batch, turn = number // ROUNDS, number % ROUNDS

        @pl.when(gz < slabs - 1)
        def _():
            send_up(batch, turn).wait_send()

        @pl.when(gz > 0)
        def _():
            send_down(batch, turn).wait_send()

        return carry

    lax.fori_loop(0, batches * ROUNDS, drain, 0)
    for batch in range(batches):
        forward(batch).wait_send()
        give_back(batch).wait()


def scatter_kernel(pairs, asked, own, vis, out, acc, sem):
    planes = acc.shape[1]
    half = planes // 2
    copies = []
    for part in range(2):
        where = pl.ds(part * half, half)
        acc[:, where] = jnp.zeros((acc.shape[0], half) + acc.shape[2:], acc.dtype)
        for batch in range(own.shape[0]):
            step = step_of(batch)
            for i in range(LANES):
                slot = half_of(batch) * LANES + i
                mine, theirs = pairs[0, step, 0, slot], asked[step, 1, slot]
                kept, returned = (theirs, mine) if batch < PUSHED else (mine, theirs)
                acc[kept, where] += own[batch, i, where]
                acc[returned, where] += vis[batch, i, where]
        copy = pltpu.make_async_copy(acc.at[:, where], out.at[:, where], sem.at[part])
        copy.start()
        copies.append(copy)
    for copy in copies:
        copy.wait()


def per_device(groups, slabs, orbitals, dielectric, pairs, pair_count):
    rows, planes, nx, ny = orbitals.shape
    pairs = jnp.swapaxes(pairs, 2, 3)
    slots = pairs.shape[3]
    orbitals, dielectric, pairs, pair_count = (
        pltpu.with_memory_space_constraint(array, pltpu.HBM)
        for array in (orbitals, dielectric, pairs, pair_count)
    )
    batches = STEPS * slots // LANES
    vmem = pl.BlockSpec(memory_space=pltpu.VMEM)
    smem = pl.BlockSpec(memory_space=pltpu.SMEM)
    hbm = pl.BlockSpec(memory_space=pltpu.HBM)
    slab = (batches, LANES, planes, nx, ny)
    halo = (batches, ROUNDS, 2, 2, nx // 2, 2 * LANES, ny)
    dma = pltpu.SemaphoreType.DMA
    own, vis, asked = pl.pallas_call(
        functools.partial(relax_kernel, groups, slabs),
        out_shape=(
            jax.ShapeDtypeStruct(slab, jnp.float32),
            jax.ShapeDtypeStruct(slab, jnp.float32),
            jax.ShapeDtypeStruct(pairs.shape[1:], jnp.int32),
        ),
        in_specs=[hbm, hbm, hbm, hbm],
        out_specs=(vmem, vmem, smem),
        scratch_shapes=[
            pltpu.VMEM(orbitals.shape, orbitals.dtype),
            pltpu.VMEM(dielectric.shape, jnp.float32),
            pltpu.SMEM(pairs.shape, jnp.int32),
            pltpu.SMEM(pair_count.shape, jnp.int32),
            pltpu.VMEM((2, 2, nx, ny), jnp.float32),
            pltpu.VMEM((planes, nx + 16, ny), jnp.float32),
            pltpu.VMEM((12, planes * nx, ny), jnp.float32),
            pltpu.VMEM((planes, nx, ny), jnp.float32),
            pltpu.VMEM(slab, jnp.bfloat16),
            pltpu.VMEM(slab, jnp.bfloat16),
            pltpu.VMEM((batches, LANES * planes * nx, ny), jnp.float32),
            pltpu.VMEM((batches, planes * nx, LANES, ny), jnp.float32),
            pltpu.VMEM((batches, 2, (planes + 4) * nx, LANES, ny), jnp.float32),
            pltpu.VMEM(halo, jnp.bfloat16),
            pltpu.VMEM(halo, jnp.bfloat16),
            pltpu.VMEM(slab, jnp.float32),
            dma((4,)),
            dma((STEPS,)),
            dma((STEPS,)),
            dma((2,)),
            dma((2,)),
            dma((batches,)),
            dma((batches,)),
            dma((batches, ROUNDS)),
            dma((batches, ROUNDS)),
            dma((batches, ROUNDS)),
            dma((batches, ROUNDS)),
            dma((batches,)),
            dma((batches,)),
        ],
        compiler_params=pltpu.CompilerParams(
            collective_id=0, has_side_effects=True, vmem_limit_bytes=48 << 20
        ),
        name="relax_pairs",
    )(orbitals, dielectric, pairs, pair_count)

    return pl.pallas_call(
        scatter_kernel,
        out_shape=jax.ShapeDtypeStruct(orbitals.shape, jnp.float32),
        in_specs=[smem, smem, vmem, vmem],
        out_specs=hbm,
        scratch_shapes=[pltpu.VMEM(orbitals.shape, jnp.float32), dma((2,))],
        compiler_params=pltpu.CompilerParams(vmem_limit_bytes=32 << 20),
        name="add_by_row",
    )(pairs, asked, own, vis)


def solution(mesh):
    placed = (
        P("orb", "gz", None, None),
        P("gz", None, None),
        P("orb", None, None, None),
        P("orb", None),
    )
    return jax.shard_map(
        functools.partial(per_device, mesh.shape["orb"], mesh.shape["gz"]),
        mesh=mesh,
        in_specs=placed,
        out_specs=P("orb", "gz", None, None),
        check_vma=False,
    )
```
